32 devices in a mesh: grp: 8 (over z, y), tm: 4 (over x, core).
Axes of the slice: x: 2, y: 2, z: 4, core: 2. Of those that a mesh axis runs over, the one named last changes fastest.
Arguments:
- voltages: bfloat16 [1024, 12, 16384], P('grp', 'tm'), may hold values from -6 to 6
Outputs:
- visibilities: float32 [2, 128, 1024, 1024], P(None, 'grp', 'tm')
The draws below stay inside these ranges and needn't reach their ends.
All inputs are finite; a program needn't handle non-finite values.
Results may differ from the reference program's by a relative error of at most 0.0053.
Values may be sent and summed in bfloat16 or wider, within the bound.
A program may use at most 192 MiB of HBM per device.

```python
import math
import jax
import jax.numpy as jnp
from jax import lax

INPUTS = 1024
CH = 128
FRAME = 16384
TAPS = 4
FRAMES = 12
FIRST = 2048


def block_levels(stream_key, shape, split, least, top_value):
    factor_of, own = 1.0, jax.random.fold_in(stream_key, 6)
    for dim, blocks in split:
        steps = jnp.exp(jax.random.uniform(jax.random.fold_in(own, dim), (blocks,), jnp.float32, least / len(split), top_value / len(split)))
        factor_of = factor_of * jnp.repeat(steps, shape[dim] // blocks).reshape([-1 if axis == dim else 1 for axis in range(len(shape))])
    return factor_of


def bell_draw(rng, shape, scale, reach, pieces=(), held_as=jnp.bfloat16):
    drawn = scale * jax.random.normal(rng, shape, jnp.float32)
    if pieces:
        drawn = drawn * block_levels(rng, shape, pieces, -0.22, 0.18)
    return jnp.clip(drawn, -reach, reach).astype(held_as)


def setup_inputs(seed: int = 0) -> dict:
    splits = jax.random.split(jax.random.key(seed), 2)
    return {
        "voltages": bell_draw(splits[0], (INPUTS, FRAMES, FRAME), 1.0, 6.0, ((0, 8), (1, 4))),
    }


def tap_table(frame_len, channels, first_bin, tap_count):
    sample = jnp.arange(frame_len, dtype=jnp.int32)
    channel = first_bin + jnp.arange(channels, dtype=jnp.int32)
    phase_index = (sample[:, None] * channel[None, :]) % frame_len
    angles = phase_index.astype(jnp.float32) * jnp.float32(2.0 * math.pi / frame_len)
    cosine = jnp.cos(angles)
    sine_vals = jnp.sin(angles)
    columns = []
    for tap_idx in range(tap_count):
        offset = ((tap_count - 1 - tap_idx) * frame_len + sample).astype(jnp.float32) + 0.5
        argument = offset / frame_len - tap_count / 2.0
        shape_part = jnp.sin(math.pi * argument) / (math.pi * argument)
        window = shape_part * (0.5 - 0.5 * jnp.cos(offset * jnp.float32(2.0 * math.pi / (tap_count * frame_len))))
        scaled = window[:, None] * (frame_len ** -0.5)
        columns.append(scaled * cosine)
        columns.append(-scaled * sine_vals)
    return jnp.concatenate(columns, axis=1).astype(jnp.bfloat16)


def filter_block(input_block, dft_table):
    block_rows, frame_total, frame_len = input_block.shape
    tapped = jnp.dot(input_block.reshape(block_rows * frame_total, frame_len), dft_table, preferred_element_type=jnp.float32)
    tapped = tapped.reshape(block_rows, frame_total, TAPS, 2 * CH)
    running = tapped[:, :, 0, :]
    for tap_idx in range(1, TAPS):
        running = running + jnp.pad(tapped[:, :frame_total - tap_idx, tap_idx, :], ((0, 0), (tap_idx, 0), (0, 0)))
    return running.astype(jnp.bfloat16)


def one_channel(parts):
    real_rows, imag_rows = parts
    real_sum = jnp.dot(real_rows.T, real_rows, precision=lax.Precision.HIGHEST) + jnp.dot(imag_rows.T, imag_rows, precision=lax.Precision.HIGHEST)
    imag_sum = jnp.dot(imag_rows.T, real_rows, precision=lax.Precision.HIGHEST) - jnp.dot(real_rows.T, imag_rows, precision=lax.Precision.HIGHEST)
    return jnp.stack([real_sum, imag_sum])


def reference(voltages):
    dft_table = tap_table(FRAME, CH, FIRST, TAPS)
    grouped = voltages.reshape(INPUTS // 32, 32, FRAMES, FRAME)
    spectra = lax.map(lambda input_block: filter_block(input_block, dft_table), grouped)
    spectra = spectra.reshape(INPUTS, FRAMES, 2 * CH)
    kept = spectra[:, TAPS - 1:, :].astype(jnp.float32)
    real_chan = jnp.transpose(kept[:, :, :CH], (2, 1, 0))
    imag_chan = jnp.transpose(kept[:, :, CH:], (2, 1, 0))
    visible = lax.map(one_channel, (real_chan, imag_chan))
    visible = jnp.transpose(visible, (1, 0, 2, 3))
    return visible * (1.0 / (FRAMES - TAPS + 1))
```

```python
import functools
import math

import jax
import jax.numpy as jnp
from jax import lax
from jax.experimental import pallas as pl
from jax.experimental.pallas import tpu as pltpu
from jax.sharding import PartitionSpec as P

CH = 128
TAPS = 4
FIRST = 2048
STEP = 128
CHUNK = 512
VMEM_LIMIT = 60 * 1024 * 1024


def phase_tables(frame_len):
    channel = FIRST + lax.broadcasted_iota(jnp.int32, (2, CH, STEP), 1)
    which = lax.broadcasted_iota(jnp.int32, (2, CH, STEP), 0)
    sample = lax.broadcasted_iota(jnp.int32, (2, CH, STEP), 2)
    index = jnp.where(which == 0, sample, STEP) * channel % frame_len
    angles = index.astype(jnp.float32) * jnp.float32(2.0 * math.pi / frame_len)
    return jnp.cos(angles), jnp.sin(angles)


def tap_windows(frame_len):
    shape = (frame_len // (2 * STEP), 2 * TAPS, STEP)
    row = lax.broadcasted_iota(jnp.int32, shape, 1)
    block = 2 * lax.broadcasted_iota(jnp.int32, shape, 0) + row // TAPS
    sample = block * STEP + lax.broadcasted_iota(jnp.int32, shape, 2)
    tap = row % TAPS
    offset = ((TAPS - 1 - tap) * frame_len + sample).astype(jnp.float32) + 0.5
    argument = offset / frame_len - TAPS / 2.0
    shape_part = jnp.sin(math.pi * argument) / (math.pi * argument)
    window = shape_part * (
        0.5 - 0.5 * jnp.cos(offset * jnp.float32(2.0 * math.pi / (TAPS * frame_len)))
    )
    return window * frame_len ** (-0.5)


def filter_kernel(v_ref, cos_ref, sin_ref, window_ref, own_ref, carry_ref, acc, even, odd, phase):
    step = pl.program_id(0)
    steps = pl.num_programs(0) - 1
    frames, in_rows, _ = v_ref.shape
    per_chunk = CHUNK // STEP

    def generate(table, chunk):
        cosine, sine = phase[0], phase[1]
        for part in range(per_chunk):
            window = window_ref[chunk * (per_chunk // 2) + part // 2]
            lanes = slice(part * STEP, (part + 1) * STEP)
            for k in range(TAPS):
                row = TAPS * (part % 2) + k
                scale = window[row : row + 1, :]
                at = 2 * CH * k
                table[at : at + CH, lanes] = (cosine * scale).astype(jnp.bfloat16)
                table[at + CH : at + 2 * CH, lanes] = (sine * -scale).astype(jnp.bfloat16)
            turn_cos, turn_sin = cos_ref[1], sin_ref[1]
            cosine, sine = cosine * turn_cos - sine * turn_sin, sine * turn_cos + cosine * turn_sin
        phase[0] = cosine
        phase[1] = sine

    def multiply(half, table):
        rows = v_ref[:, :, half * CHUNK : (half + 1) * CHUNK].reshape(frames * in_rows, CHUNK)
        acc[...] += lax.dot_general(
            rows, table[...], (((1,), (1,)), ((), ())), preferred_element_type=jnp.float32
        )

    @pl.when(step == 0)
    def _():
        acc[...] = jnp.zeros_like(acc)
        phase[0] = cos_ref[0]
        phase[1] = sin_ref[0]
        generate(even, 0)

    @pl.when(step < steps)
    def _():
        multiply(0, even)
        generate(odd, 2 * step + 1)
        multiply(1, odd)
        generate(even, jnp.minimum(2 * step + 2, 2 * steps - 1))

    @pl.when(step == steps)
    def _():
        warmup = TAPS - 1
        for f in range(frames + warmup):
            total = None
            for k in range(TAPS):
                if 0 <= f - k < frames:
                    piece = acc[(f - k) * in_rows : (f - k + 1) * in_rows, 2 * CH * k : 2 * CH * (k + 1)]
                    total = piece if total is None else total + piece
            turned = total.T
            if f < frames:
                own_ref[f] = turned.reshape(own_ref.shape[1:])
            else:
                carry_ref[f - frames] = turned.reshape(carry_ref.shape[1:])


def filter_bank(voltages, groups):
    in_rows, frames, frame_len = voltages.shape
    by_frame = jnp.transpose(voltages, (1, 0, 2))
    cosines, sines = phase_tables(frame_len)
    windows = tap_windows(frame_len)
    steps = frame_len // (2 * CHUNK)
    warmup = TAPS - 1
    tail = (2, groups, CH // groups, in_rows)
    whole = lambda x: pl.BlockSpec(x.shape, lambda i: (0,) * x.ndim)
    return pl.pallas_call(
        filter_kernel,
        grid=(steps + 1,),
        out_shape=(
            jax.ShapeDtypeStruct((frames, *tail), jnp.float32),
            jax.ShapeDtypeStruct((warmup, *tail), jnp.float32),
        ),
        in_specs=[
            pl.BlockSpec((frames, in_rows, 2 * CHUNK), lambda i: (0, 0, jnp.minimum(i, steps - 1))),
            whole(cosines),
            whole(sines),
            whole(windows),
        ],
        out_specs=(
            pl.BlockSpec((frames, *tail), lambda i: (0,) * 5),
            pl.BlockSpec((warmup, *tail), lambda i: (0,) * 5),
        ),
        scratch_shapes=[
            pltpu.VMEM((frames * in_rows, 2 * CH * TAPS), jnp.float32),
            pltpu.VMEM((2 * CH * TAPS, CHUNK), jnp.bfloat16),
            pltpu.VMEM((2 * CH * TAPS, CHUNK), jnp.bfloat16),
            pltpu.VMEM((2, CH, STEP), jnp.float32),
        ],
        compiler_params=pltpu.CompilerParams(vmem_limit_bytes=VMEM_LIMIT),
        name="filter_bank",
    )(by_frame, cosines, sines, windows)


def cross_kernel(depth, scale, spectra_ref, out_ref, right, left):
    channel = pl.program_id(0)
    times, groups, frames, _, channels, in_rows = spectra_ref.shape
    row_count = out_ref.shape[2]
    warmup = TAPS - 1
    halves, padded = right.shape[0], right.shape[1]

    @pl.when(channel == 0)
    def _():
        for half in range(halves):
            for g in range(groups):
                pieces = []
                for p in range(2):
                    for f in range(warmup, times * frames):
                        tile = spectra_ref[f // frames, g, f % frames, p].astype(jnp.float32)
                        pieces.append(tile[8 * half : 8 * half + 8])
                if padded > depth:
                    pieces.append(jnp.zeros((padded - depth, in_rows), jnp.float32))
                right[half, :, g * in_rows : (g + 1) * in_rows] = jnp.concatenate(pieces).astype(jnp.bfloat16)
            start = pl.multiple_of(lax.axis_index("tm") * row_count, 128)
            own = right[half, :, pl.ds(start, row_count)].astype(jnp.float32)
            left[half, 0] = own.T
            swapped = [own[depth // 2 : depth], -own[: depth // 2]]
            if padded > depth:
                swapped.append(own[depth:])
            left[half, 1] = jnp.concatenate(swapped).T

    half = channel // 8
    lane = lax.broadcasted_iota(jnp.int32, (row_count, padded), 1)
    chosen = lane % 8 == channel % 8
    for p in range(2):
        rows = jnp.where(chosen, left[half, p], 0.0).astype(jnp.bfloat16)
        out_ref[p, 0] = jnp.dot(rows, right[half], preferred_element_type=jnp.float32) * scale


def cross_multiply(spectra, row_count):
    times, groups, frames, _, channels, in_rows = spectra.shape
    kept = times * frames - (TAPS - 1)
    depth = 2 * kept * 8
    padded = -(-depth // 128) * 128
    halves = channels // 8
    return pl.pallas_call(
        functools.partial(cross_kernel, depth, 1.0 / kept),
        grid=(channels,),
        out_shape=jax.ShapeDtypeStruct((2, channels, row_count, groups * in_rows), jnp.float32),
        in_specs=[pl.BlockSpec(spectra.shape, lambda c: (0,) * 6)],
        out_specs=pl.BlockSpec((2, 1, row_count, groups * in_rows), lambda c: (0, c, 0, 0)),
        scratch_shapes=[
            pltpu.VMEM((halves, padded, groups * in_rows), jnp.bfloat16),
            pltpu.VMEM((halves, 2, row_count, padded), jnp.float32),
        ],
        compiler_params=pltpu.CompilerParams(vmem_limit_bytes=VMEM_LIMIT),
        name="cross_multiply",
    )(spectra)


def local(voltages):
    in_rows, frames, _ = voltages.shape
    groups, times = lax.axis_size("grp"), lax.axis_size("tm")
    own, carry = filter_bank(voltages, groups)
    carried = lax.ppermute(carry, "tm", [(i, i + 1) for i in range(times - 1)])
    first = own[: TAPS - 1] + carried
    spectra = jnp.concatenate([first, own[TAPS - 1 :]]).astype(jnp.bfloat16)
    turned = lax.all_to_all(spectra, "grp", split_axis=2, concat_axis=0)
    gathered = lax.all_gather(turned, "tm", axis=0)
    return cross_multiply(gathered, in_rows * groups // times)


def solution(mesh):
    return jax.shard_map(
        local,
        mesh=mesh,
        in_specs=(P("grp", "tm", None),),
        out_specs=P(None, "grp", "tm", None),
        check_vma=False,
    )
```

```python
import functools
import math

import jax
import jax.numpy as jnp
from jax import lax
from jax.experimental import pallas as pl
from jax.experimental.pallas import tpu as pltpu
from jax.sharding import PartitionSpec as P

CH = 128
TAPS = 4
FIRST = 2048
STEP = 128
CHUNK = 512
VMEM_LIMIT = 60 * 1024 * 1024


def phase_tables(frame_len):
    channel = FIRST + lax.broadcasted_iota(jnp.int32, (2, CH, STEP), 1)
    which = lax.broadcasted_iota(jnp.int32, (2, CH, STEP), 0)
    sample = lax.broadcasted_iota(jnp.int32, (2, CH, STEP), 2)
    index = jnp.where(which == 0, sample, STEP) * channel % frame_len
    angles = index.astype(jnp.float32) * jnp.float32(2.0 * math.pi / frame_len)
    return jnp.cos(angles), jnp.sin(angles)


def tap_windows(frame_len):
    shape = (frame_len // (2 * STEP), 2 * TAPS, STEP)
    row = lax.broadcasted_iota(jnp.int32, shape, 1)
    block = 2 * lax.broadcasted_iota(jnp.int32, shape, 0) + row // TAPS
    sample = block * STEP + lax.broadcasted_iota(jnp.int32, shape, 2)
    tap = row % TAPS
    offset = ((TAPS - 1 - tap) * frame_len + sample).astype(jnp.float32) + 0.5
    argument = offset / frame_len - TAPS / 2.0
    shape_part = jnp.sin(math.pi * argument) / (math.pi * argument)
    window = shape_part * (
        0.5 - 0.5 * jnp.cos(offset * jnp.float32(2.0 * math.pi / (TAPS * frame_len)))
    )
    return window * frame_len ** (-0.5)


def filter_kernel(v_ref, cos_ref, sin_ref, window_ref, own_ref, carry_ref, acc, even, odd, phase):
    step = pl.program_id(0)
    steps = pl.num_programs(0) - 1
    frames, in_rows, _ = v_ref.shape
    per_chunk = CHUNK // STEP

    def generate(table, chunk):
        cosine, sine = phase[0], phase[1]
        for part in range(per_chunk):
            window = window_ref[chunk * (per_chunk // 2) + part // 2]
            lanes = slice(part * STEP, (part + 1) * STEP)
            for k in range(TAPS):
                row = TAPS * (part % 2) + k
                scale = window[row : row + 1, :]
                at = 2 * CH * k
                table[at : at + CH, lanes] = (cosine * scale).astype(jnp.bfloat16)
                table[at + CH : at + 2 * CH, lanes] = (sine * -scale).astype(jnp.bfloat16)
            turn_cos, turn_sin = cos_ref[1], sin_ref[1]
            cosine, sine = cosine * turn_cos - sine * turn_sin, sine * turn_cos + cosine * turn_sin
        phase[0] = cosine
        phase[1] = sine

    def multiply(half, table):
        rows = v_ref[:, :, half * CHUNK : (half + 1) * CHUNK].reshape(frames * in_rows, CHUNK)
        acc[...] += lax.dot_general(
            rows, table[...], (((1,), (1,)), ((), ())), preferred_element_type=jnp.float32
        )

    @pl.when(step == 0)
    def _():
        acc[...] = jnp.zeros_like(acc)
        phase[0] = cos_ref[0]
        phase[1] = sin_ref[0]
        generate(even, 0)

    @pl.when(step < steps)
    def _():
        multiply(0, even)
        generate(odd, 2 * step + 1)
        multiply(1, odd)
        generate(even, jnp.minimum(2 * step + 2, 2 * steps - 1))

    @pl.when(step == steps)
    def _():
        warmup = TAPS - 1
        for f in range(frames + warmup):
            total = None
            for k in range(TAPS):
                if 0 <= f - k < frames:
                    piece = acc[(f - k) * in_rows : (f - k + 1) * in_rows, 2 * CH * k : 2 * CH * (k + 1)]
                    total = piece if total is None else total + piece
            turned = total.T
            if f < frames:
                own_ref[f] = turned.reshape(own_ref.shape[1:])
            else:
                carry_ref[f - frames] = turned.reshape(carry_ref.shape[1:]).astype(jnp.bfloat16)


def filter_bank(voltages, groups):
    in_rows, frames, frame_len = voltages.shape
    by_frame = jnp.transpose(voltages, (1, 0, 2))
    cosines, sines = phase_tables(frame_len)
    windows = tap_windows(frame_len)
    steps = frame_len // (2 * CHUNK)
    warmup = TAPS - 1
    tail = (2, groups, CH // groups, in_rows)
    whole = lambda x: pl.BlockSpec(x.shape, lambda i: (0,) * x.ndim)
    return pl.pallas_call(
        filter_kernel,
        grid=(steps + 1,),
        out_shape=(
            jax.ShapeDtypeStruct((frames, *tail), jnp.float32),
            jax.ShapeDtypeStruct((warmup, *tail), jnp.bfloat16),
        ),
        in_specs=[
            pl.BlockSpec((frames, in_rows, 2 * CHUNK), lambda i: (0, 0, jnp.minimum(i, steps - 1))),
            whole(cosines),
            whole(sines),
            whole(windows),
        ],
        out_specs=(
            pl.BlockSpec((frames, *tail), lambda i: (0,) * 5),
            pl.BlockSpec((warmup, *tail), lambda i: (0,) * 5),
        ),
        scratch_shapes=[
            pltpu.VMEM((frames * in_rows, 2 * CH * TAPS), jnp.float32),
            pltpu.VMEM((2 * CH * TAPS, CHUNK), jnp.bfloat16),
            pltpu.VMEM((2 * CH * TAPS, CHUNK), jnp.bfloat16),
            pltpu.VMEM((2, CH, STEP), jnp.float32),
        ],
        compiler_params=pltpu.CompilerParams(vmem_limit_bytes=VMEM_LIMIT),
        name="filter_bank",
    )(by_frame, cosines, sines, windows)


def cross_kernel(depth, scale, spectra_ref, out_ref, right, left):
    channel = pl.program_id(0)
    times, groups, frames, _, channels, in_rows = spectra_ref.shape
    row_count = out_ref.shape[2]
    warmup = TAPS - 1
    halves, padded = right.shape[0], right.shape[1]

    @pl.when(channel == 0)
    def _():
        for half in range(halves):
            for g in range(groups):
                pieces = []
                for p in range(2):
                    for f in range(warmup, times * frames):
                        tile = spectra_ref[f // frames, g, f % frames, p].astype(jnp.float32)
                        pieces.append(tile[8 * half : 8 * half + 8])
                if padded > depth:
                    pieces.append(jnp.zeros((padded - depth, in_rows), jnp.float32))
                right[half, :, g * in_rows : (g + 1) * in_rows] = jnp.concatenate(pieces).astype(jnp.bfloat16)
            start = pl.multiple_of(lax.axis_index("tm") * row_count, 128)
            own = right[half, :, pl.ds(start, row_count)].astype(jnp.float32)
            left[half, 0] = own.T
            swapped = [own[depth // 2 : depth], -own[: depth // 2]]
            if padded > depth:
                swapped.append(own[depth:])
            left[half, 1] = jnp.concatenate(swapped).T

    half = channel // 8
    lane = lax.broadcasted_iota(jnp.int32, (row_count, padded), 1)
    chosen = lane % 8 == channel % 8
    for p in range(2):
        rows = jnp.where(chosen, left[half, p], 0.0).astype(jnp.bfloat16)
        out_ref[p, 0] = jnp.dot(rows, right[half], preferred_element_type=jnp.float32) * scale


def cross_multiply(spectra, row_count):
    times, groups, frames, _, channels, in_rows = spectra.shape
    kept = times * frames - (TAPS - 1)
    depth = 2 * kept * 8
    padded = -(-depth // 128) * 128
    halves = channels // 8
    return pl.pallas_call(
        functools.partial(cross_kernel, depth, 1.0 / kept),
        grid=(channels,),
        out_shape=jax.ShapeDtypeStruct((2, channels, row_count, groups * in_rows), jnp.float32),
        in_specs=[pl.BlockSpec(spectra.shape, lambda c: (0,) * 6)],
        out_specs=pl.BlockSpec((2, 1, row_count, groups * in_rows), lambda c: (0, c, 0, 0)),
        scratch_shapes=[
            pltpu.VMEM((halves, padded, groups * in_rows), jnp.bfloat16),
            pltpu.VMEM((halves, 2, row_count, padded), jnp.float32),
        ],
        compiler_params=pltpu.CompilerParams(vmem_limit_bytes=VMEM_LIMIT),
        name="cross_multiply",
    )(spectra)


def spread_kernel(
    own_ref, carry_ref, out_ref, carried, send, local_sem, carry_sems, group_sems, partner_sems, row_sems, relay_sems
):
    frames, _, groups = own_ref.shape[:3]
    times = out_ref.shape[0]
    pairs = times // 2
    warmup = TAPS - 1
    unused = warmup // frames
    g, t = lax.axis_index("grp"), lax.axis_index("tm")
    partner = t + 1 - 2 * lax.rem(t, 2)

    def copy(src, dst, sems, at, device):
        return pltpu.make_async_remote_copy(
            src_ref=src,
            dst_ref=dst,
            send_sem=sems.at[(0, *at)],
            recv_sem=sems.at[(1, *at)],
            device_id=device,
            device_id_type=pl.DeviceIdType.MESH,
        )

    barrier = pltpu.get_barrier_semaphore()
    for d in range(1, groups):
        pl.semaphore_signal(
            barrier, inc=1, device_id=(lax.rem(g + d, groups), t), device_id_type=pl.DeviceIdType.MESH
        )
    for d in range(1, times):
        pl.semaphore_signal(
            barrier, inc=1, device_id=(g, lax.rem(t + d, times)), device_id_type=pl.DeviceIdType.MESH
        )
    pl.semaphore_wait(barrier, groups + times - 2)

    carry_copy = copy(carry_ref, carried, carry_sems, (), (g, lax.rem(t + 1, times)))

    @pl.when(t < times - 1)
    def _():
        carry_copy.start()

    @pl.when(t > 0)
    def _():
        carry_copy.wait_recv()

    @pl.when(t == 0)
    def _():
        carried[...] = jnp.zeros_like(carried)

    for f in range(frames):
        for p in range(2):
            total = own_ref[f, p]
            if f < warmup:
                total = total + carried[f, p].astype(jnp.float32)
            send[:, f, p] = total.astype(jnp.bfloat16)
    keep = pltpu.make_async_copy(send.at[g], out_ref.at[t, g], local_sem)
    keep.start()
    keep.wait()

    def source(d):
        return lax.rem(g + groups - d, groups)

    def other(at, e):
        return lax.rem(at + times - 2 * e, times)

    def to_group(d):
        to = lax.rem(g + d, groups)
        return copy(send.at[to], out_ref.at[t, g], group_sems, (d,), (to, t))

    def to_partner(d):
        block = out_ref.at[t, source(d)]
        return copy(block, block, partner_sems, (d,), (g, partner))

    def to_row(e, d):
        block = out_ref.at[t, source(d)]
        return copy(block, block, row_sems, (e, d), (g, lax.rem(t + 2 * e, times)))

    def relayed(e, d):
        block = out_ref.at[other(t, e), source(d)]
        return copy(block, block, relay_sems, (e, d), (g, partner))

    @pl.when(t >= unused)
    def _():
        for d in range(1, groups):
            to_group(d).start()
        for d in range(groups):
            if d:
                to_group(d).wait_recv()
            for e in range(1, pairs):
                to_row(e, d).start()
            to_partner(d).start()

    for e in range(1, pairs):

        @pl.when(other(t, e) >= unused)
        def _(e=e):
            for d in range(groups):
                to_row(e, d).wait_recv()
                relayed(e, d).start()

    @pl.when(partner >= unused)
    def _():
        for d in range(groups):
            to_partner(d).wait_recv()

    for e in range(1, pairs):

        @pl.when(other(partner, e) >= unused)
        def _(e=e):
            for d in range(groups):
                relayed(e, d).wait_recv()

        @pl.when(other(t, e) >= unused)
        def _(e=e):
            for d in range(groups):
                relayed(e, d).wait_send()

    @pl.when(t >= unused)
    def _():
        for d in range(groups):
            if d:
                to_group(d).wait_send()
            to_partner(d).wait_send()
            for e in range(1, pairs):
                to_row(e, d).wait_send()

    @pl.when(t < times - 1)
    def _():
        carry_copy.wait_send()


def spread(own, carry):
    frames, parts, groups, channels, in_rows = own.shape
    times = lax.axis_size("tm")
    vmem = pl.BlockSpec(memory_space=pltpu.VMEM)
    return pl.pallas_call(
        spread_kernel,
        out_shape=jax.ShapeDtypeStruct((times, groups, frames, parts, channels, in_rows), jnp.bfloat16),
        in_specs=[vmem, vmem],
        out_specs=vmem,
        scratch_shapes=[
            pltpu.VMEM(carry.shape, carry.dtype),
            pltpu.VMEM((groups, frames, parts, channels, in_rows), jnp.bfloat16),
            pltpu.SemaphoreType.DMA,
            pltpu.SemaphoreType.DMA((2,)),
            pltpu.SemaphoreType.DMA((2, groups)),
            pltpu.SemaphoreType.DMA((2, groups)),
            pltpu.SemaphoreType.DMA((2, times // 2, groups)),
            pltpu.SemaphoreType.DMA((2, times // 2, groups)),
        ],
        compiler_params=pltpu.CompilerParams(
            collective_id=0, has_side_effects=True, vmem_limit_bytes=VMEM_LIMIT
        ),
        name="spread",
    )(own, carry)


def local(voltages):
    in_rows, _, _ = voltages.shape
    groups, times = lax.axis_size("grp"), lax.axis_size("tm")
    own, carry = filter_bank(voltages, groups)
    return cross_multiply(spread(own, carry), in_rows * groups // times)


def solution(mesh):
    return jax.shard_map(
        local,
        mesh=mesh,
        in_specs=(P("grp", "tm", None),),
        out_specs=P(None, "grp", "tm", None),
        check_vma=False,
    )
```
